32 devices in a mesh: dp: 8 (over y, x, core), mp: 4 (over z).
Axes of the slice: x: 2, y: 2, z: 4, core: 2. Of those that a mesh axis runs over, the one named last changes fastest.
Arguments:
- patches: bfloat16 [8192, 1024], P(('dp', 'mp')), as said below
- scene_ids: int32 [8192], P(('dp', 'mp')), may hold values from 0 to 7, as said below
- owner_ids: int32 [8192], P(('dp', 'mp')), may hold values from 0 to 7, as said below
- fill_slot: int32 [32768], P(('dp', 'mp')), may hold values from -1 to 511, as said below
- norm1_gain: float32 [1024], replicated, may hold values from 0.1 to 1.9
- norm1_bias: float32 [1024], replicated, may hold values from -1.75 to 1.75
- qkv_weight: bfloat16 [1024, 3, 1024], P(None, None, 'mp'), may hold values from -0.25 to 0.25
- qv_bias: float32 [2, 1024], P(None, 'mp'), may hold values from -3 to 3
- out_weight: bfloat16 [1024, 1024], P('mp'), may hold values from -1.5 to 1.5
- out_bias: float32 [1024], replicated, may hold values from -1.75 to 1.75
- norm2_gain: float32 [1024], replicated, may hold values from 0.1 to 1.9
- norm2_bias: float32 [1024], replicated, may hold values from -1.75 to 1.75
- up_weight: bfloat16 [1024, 4096], P(None, 'mp'), may hold values from -0.1875 to 0.1875
- up_bias: bfloat16 [4096], P('mp'), may hold values from -3 to 3
- down_weight: bfloat16 [4096, 1024], P('mp'), may hold values from -0.125 to 0.125
- down_bias: float32 [1024], replicated, may hold values from -1.75 to 1.75
- dec_weight: bfloat16 [1024, 512], replicated, may hold values from -0.1875 to 0.1875
- dec_bias: float32 [512], replicated, may hold values from -1.75 to 1.75
- mask_token: float32 [512], replicated, may hold values from -6 to 6
- positions: bfloat16 [32768, 512], P(('dp', 'mp')), may hold values from -6 to 6
- cotangent: bfloat16 [32768, 512], P(('dp', 'mp')), may hold values from -6 to 6
Outputs:
- decoder_in: bfloat16 [32768, 512], P(('dp', 'mp'))
- grad_patches: float32 [8192, 1024], P(('dp', 'mp'))
- grad_norm1_gain: float32 [1024], replicated
- grad_norm1_bias: float32 [1024], replicated
- grad_qkv_weight: float32 [1024, 3, 1024], P(None, None, 'mp')
- grad_qv_bias: float32 [2, 1024], P(None, 'mp')
- grad_out_weight: float32 [1024, 1024], P('mp')
- grad_out_bias: float32 [1024], replicated
- grad_norm2_gain: float32 [1024], replicated
- grad_norm2_bias: float32 [1024], replicated
- grad_up_weight: float32 [1024, 4096], P(None, 'mp')
- grad_up_bias: float32 [4096], P('mp')
- grad_down_weight: float32 [4096, 1024], P('mp')
- grad_down_bias: float32 [1024], replicated
- grad_dec_weight: float32 [1024, 512], replicated
- grad_dec_bias: float32 [512], replicated
- grad_mask_token: float32 [512], replicated
The draws below stay inside these ranges and needn't reach their ends.
Inputs may be any that keep to these rules, and one draw needn't show every extreme that they name: `scene_ids`: within each group of 1024 rows (one dp index) scene ids start at 0 and rise by one at each scene boundary, never falling; scene 0 holds 256 to 512 rows, every other scene at least one. `owner_ids`: among the 256 rows of one device no owner is named more than 64 times; in each mp column one owner is named exactly 64 times by the rows of every device. `fill_slot`: in grid block e, slot s * 64 + r is named by exactly one cell when device (s, e % 4) has an r-th row (in row order) with owner e // 4, and by no cell otherwise. `patches`: magnitudes stay below 200.
All inputs are finite; a program needn't handle non-finite values.
Results may differ from the reference program's by a relative error of at most 0.013.
The reference program's roundings to bfloat16 on the way count: a program that leaves them out, or rounds other values in their place, can miss the bound.
Values may be sent and summed in bfloat16 or wider, within the bound.
A program may use at most 128 MiB of HBM per device.

```python
import jax
import jax.numpy as jnp
from jax import lax

D = 1024
HEADS = 16
HEAD_DIM = 64
FF = 4096
DEC = 512
ROWS = 256
SEGS = 8
GROUP_ROWS = 1024
TOKENS = 8192
CAP = 64
SLOTS = 512
GRID = 1024
N_DP = 8
N_MP = 4


def draw_patches(key, part):
    key_center, key_jitter, key_column, key_rowscale = jax.random.split(jax.random.fold_in(key, 11), 4)
    row_place = jnp.arange(TOKENS, dtype=jnp.float32) / TOKENS
    rising = jnp.exp(jnp.log(3.0) * row_place)[:, None]
    column = jnp.exp(jax.random.uniform(key_column, (1, D), minval=jnp.log(0.3), maxval=jnp.log(3.0)))
    center = jax.random.normal(key_center, (1, D))
    rowscale = jnp.exp(jax.random.uniform(key_rowscale, (TOKENS, 1), minval=0.0, maxval=jnp.log(4.0)))
    jitter = jnp.clip(jax.random.normal(key_jitter, (TOKENS, D)), -4.0, 4.0)
    center = jnp.clip(center, -3.0, 3.0)
    return ((center * rising + jitter * rising * rowscale) * column).astype(jnp.bfloat16)


def draw_scene_ids(key, part):
    groups = TOKENS // GROUP_ROWS

    def one_group(group_key):
        key_first, key_cuts = jax.random.split(group_key)
        first_scene = jax.random.randint(key_first, (), GROUP_ROWS // 4, GROUP_ROWS // 2 + 1)
        remaining = GROUP_ROWS - first_scene
        shuffled = jax.random.permutation(key_cuts, GROUP_ROWS).astype(jnp.int32)
        order_key = jnp.where(shuffled < remaining - 1, jnp.arange(GROUP_ROWS, dtype=jnp.int32), GROUP_ROWS + jnp.arange(GROUP_ROWS, dtype=jnp.int32))
        picked = jnp.argsort(order_key)[:SEGS - 2]
        cut_points = shuffled[picked] + 1
        where_rows = jnp.arange(GROUP_ROWS, dtype=jnp.int32)
        offset_rows = where_rows - first_scene
        later = 1 + jnp.sum((cut_points[None, :] <= offset_rows[:, None]).astype(jnp.int32), axis=1)
        return jnp.where(where_rows < first_scene, 0, later).astype(jnp.int32)
    keys_all = jax.random.split(jax.random.fold_in(key, 5), groups)
    return jax.vmap(one_group)(keys_all).reshape(TOKENS).astype(jnp.int32)


def routing_tables(key):
    key_star, key_blocks, key_rows, key_cells = jax.random.split(jax.random.fold_in(key, 7), 4)
    blocks = N_DP * N_MP
    star = jax.random.randint(key_star, (N_MP,), 0, N_DP)

    def block_counts(block_key, block_index):
        key_order, key_share = jax.random.split(block_key)
        order = jnp.concatenate([jnp.zeros((1,), jnp.int32), 1 + jax.random.permutation(key_order, N_DP - 1).astype(jnp.int32)])
        owners = (star[block_index % N_MP] + order) % N_DP
        share = jax.random.randint(key_share, (N_DP // 2,), 0, CAP + 1)
        share = share.at[0].set(CAP)
        amounts = jnp.stack([share, CAP - share], axis=1).reshape(N_DP)
        return jnp.zeros((N_DP,), jnp.int32).at[owners].set(amounts)
    counts = jax.vmap(block_counts)(jax.random.split(key_blocks, blocks), jnp.arange(blocks, dtype=jnp.int32))

    def block_owner(row_key, count_row):
        bounds = jnp.cumsum(count_row)
        sorted_owner = jnp.sum((bounds[None, :] <= jnp.arange(ROWS, dtype=jnp.int32)[:, None]).astype(jnp.int32), axis=1)
        return sorted_owner[jax.random.permutation(row_key, ROWS)]
    owner_all = jax.vmap(block_owner)(jax.random.split(key_rows, blocks), counts).reshape(TOKENS)

    def grid_fill(cell_key, grid_index):
        owner_dp = grid_index // N_MP
        column_mp = grid_index % N_MP
        senders = counts.reshape(N_DP, N_MP, N_DP)[:, column_mp, owner_dp]
        valid = jnp.arange(CAP, dtype=jnp.int32)[None, :] < senders[:, None]
        flat_valid = valid.reshape(-1).astype(jnp.int32)
        order = jnp.cumsum(flat_valid) - 1
        cells = jax.random.permutation(cell_key, GRID).astype(jnp.int32)
        target = jnp.where(flat_valid > 0, cells[jnp.maximum(order, 0)], GRID)
        slot_ids = jnp.arange(N_DP * CAP, dtype=jnp.int32)
        return jnp.full((GRID + 1,), -1, jnp.int32).at[target].set(slot_ids)[:GRID]
    fill_all = jax.vmap(grid_fill)(jax.random.split(key_cells, blocks), jnp.arange(blocks, dtype=jnp.int32)).reshape(blocks * GRID)
    return (owner_all.astype(jnp.int32), fill_all.astype(jnp.int32))


def draw_owner_ids(key, part):
    return routing_tables(key)[0]


def draw_fill_slot(key, part):
    return routing_tables(key)[1]


def shard_levels(stream_key, shape, shards, least, high):
    def one(axis_at, blocks):
        heights = jax.random.uniform(jax.random.fold_in(jax.random.fold_in(stream_key, 6), axis_at), (blocks,), jnp.float32, least / len(shards), high / len(shards))
        return jnp.repeat(jnp.exp(heights), shape[axis_at] // blocks).reshape((-1,) + (1,) * (len(shape) - axis_at - 1))

    level = one(*shards[0])
    for cut in shards[1:]:
        level = level * one(*cut)
    return level


def centred(stream_key, dims, scale, limit, pieces=(), kind=jnp.bfloat16):
    factor_of = shard_levels(stream_key, dims, pieces, -0.22, 0.18) if pieces else 1.0
    result = jax.random.normal(stream_key, dims, jnp.float32) * scale * factor_of
    return jnp.minimum(jnp.maximum(result, -limit), limit).astype(kind)


def setup_inputs(seed: int = 0) -> dict:
    arg_keys = jax.random.split(jax.random.key(seed), 22)
    return {
        "patches": draw_patches(jax.random.fold_in(arg_keys[21], 71), 0),
        "scene_ids": draw_scene_ids(jax.random.fold_in(arg_keys[21], 71), 0),
        "owner_ids": draw_owner_ids(jax.random.fold_in(arg_keys[21], 71), 0),
        "fill_slot": draw_fill_slot(jax.random.fold_in(arg_keys[21], 71), 0),
        "norm1_gain": jnp.clip(1.0 + 0.18 * jax.random.normal(arg_keys[4], (D,), jnp.float32), 0.1, 1.9),
        "norm1_bias": centred(arg_keys[5], (D,), 0.3, 1.75, (), jnp.float32),
        "qkv_weight": centred(arg_keys[6], (D, 3, D), (D // 2) ** -0.5, 0.25, ((2, 4),)),
        "qv_bias": centred(arg_keys[7], (2, D), 0.5, 3.0, ((1, 4),), jnp.float32),
        "out_weight": centred(arg_keys[8], (D, D), (D // 64) ** -0.5, 1.5, ((0, 4),)),
        "out_bias": centred(arg_keys[9], (D,), 0.3, 1.75, (), jnp.float32),
        "norm2_gain": jnp.clip(1.0 + 0.18 * jax.random.normal(arg_keys[10], (D,), jnp.float32), 0.1, 1.9),
        "norm2_bias": centred(arg_keys[11], (D,), 0.3, 1.75, (), jnp.float32),
        "up_weight": centred(arg_keys[12], (D, FF), D ** -0.5, 0.1875, ((1, 4),)),
        "up_bias": centred(arg_keys[13], (FF,), 0.5, 3.0, ((0, 4),)),
        "down_weight": centred(arg_keys[14], (FF, D), (FF // 2) ** -0.5, 0.125, ((0, 4),)),
        "down_bias": centred(arg_keys[15], (D,), 0.3, 1.75, (), jnp.float32),
        "dec_weight": centred(arg_keys[16], (D, DEC), D ** -0.5, 0.1875),
        "dec_bias": centred(arg_keys[17], (DEC,), 0.3, 1.75, (), jnp.float32),
        "mask_token": centred(arg_keys[18], (DEC,), 1.0, 6.0, (), jnp.float32),
        "positions": centred(arg_keys[19], (N_DP * N_MP * GRID, DEC), 1.0, 6.0, ((0, 32),)),
        "cotangent": centred(arg_keys[20], (N_DP * N_MP * GRID, DEC), 1.0, 6.0, ((0, 32),)),
    }


HIGH = lax.Precision.HIGHEST

@jax.custom_vjp
def low(v):
    return lax.optimization_barrier(v.astype(jnp.bfloat16)).astype(jnp.float32)

@jax.custom_vjp
def low_back(v):
    return v

def low_keep(v):
    return (low(v), None)

def low_pass(kept, grad):
    return (grad,)

def back_keep(v):
    return (v, None)

def back_low(kept, grad):
    return (low(grad),)
low.defvjp(low_keep, low_pass)
low_back.defvjp(back_keep, back_low)

def layer_norm(hidden, gain, bias_vec):
    centered = hidden - lax.optimization_barrier(jnp.mean(hidden, axis=-1, keepdims=True))
    spread = lax.optimization_barrier(jnp.mean(centered * centered, axis=-1, keepdims=True))
    return centered * lax.rsqrt(spread + 1e-06) * gain + bias_vec

def attend_head(packed):
    triple, scenes = packed
    queries = triple[0]
    keys_all = triple[1]
    values = triple[2]
    scores = jnp.dot(queries, keys_all.T, precision=HIGH) * HEAD_DIM ** (-0.5)
    scores = low_back(scores)
    scores = jnp.where(scenes[:, None] == scenes[None, :], scores, -1000000000.0)
    softmax_w = low(jax.nn.softmax(scores, axis=-1))
    return jnp.dot(softmax_w, values, precision=HIGH)

def reference(patches, scene_ids, owner_ids, fill_slot, norm1_gain, norm1_bias, qkv_weight, qv_bias, out_weight, out_bias, norm2_gain, norm2_bias, up_weight, up_bias, down_weight, down_bias, dec_weight, dec_bias, mask_token, positions, cotangent):
    devices = N_DP * N_MP
    groups = TOKENS // GROUP_ROWS
    owner_rows = owner_ids.reshape(devices, ROWS)
    owner_onehot = (owner_rows[:, :, None] == jnp.arange(N_DP, dtype=jnp.int32)[None, None, :]).astype(jnp.int32)
    earlier = lax.optimization_barrier(jnp.sum((jnp.cumsum(owner_onehot, axis=1) - owner_onehot) * owner_onehot, axis=2))
    block_ids = jnp.arange(devices, dtype=jnp.int32)[:, None]
    recv_slot = block_ids // N_MP * CAP + earlier
    dest_block = owner_rows * N_MP + block_ids % N_MP
    token_table = jnp.zeros((devices, SLOTS), jnp.int32).at[dest_block.reshape(-1), recv_slot.reshape(-1)].set(jnp.arange(TOKENS, dtype=jnp.int32))
    fill_grid = fill_slot.reshape(devices, GRID)
    filled = (fill_grid >= 0).reshape(-1, 1)
    source = jnp.take_along_axis(token_table, jnp.maximum(fill_grid, 0), axis=1).reshape(-1)
    scene_heads = jnp.repeat(scene_ids.reshape(groups, GROUP_ROWS), HEADS, axis=0)
    position_f = positions.astype(jnp.float32)

    def forward(inputs, gain_one, bias_one, qkv_w, qv_b, out_w, out_b, gain_two, bias_two, up_w, up_b, down_w, down_b, dec_w, dec_b, mask_vec):
        band_mean = lax.optimization_barrier(jnp.mean(inputs, axis=0))
        band_var = lax.optimization_barrier(jnp.mean(inputs * inputs, axis=0)) - band_mean * band_mean
        band_hat = (inputs - band_mean) * lax.rsqrt(band_var + 1e-05)
        normed1 = low(layer_norm(band_hat, gain_one, bias_one))
        bias_three = jnp.stack([qv_b[0], jnp.zeros_like(qv_b[0]), qv_b[1]])
        triples = jnp.einsum('td,dcj->tcj', normed1, qkv_w, precision=HIGH) + bias_three
        triples = low(low_back(triples))
        per_head = triples.reshape(groups, GROUP_ROWS, 3, HEADS, HEAD_DIM).transpose(0, 3, 2, 1, 4).reshape(groups * HEADS, 3, GROUP_ROWS, HEAD_DIM)
        attended = lax.map(jax.checkpoint(attend_head), (per_head, scene_heads))
        heads_out = attended.reshape(groups, HEADS, GROUP_ROWS, HEAD_DIM).transpose(0, 2, 1, 3).reshape(TOKENS, D)
        heads_out = low(low_back(heads_out))
        attn_out = low_back(jnp.dot(heads_out, out_w, precision=HIGH) + out_b)
        after_attn = band_hat + attn_out
        normed2 = low(layer_norm(after_attn, gain_two, bias_two))
        pre_act = low_back(jnp.dot(normed2, up_w, precision=HIGH) + up_b)
        activated = low(jax.nn.gelu(pre_act, approximate=False))
        mlp_out = low_back(jnp.dot(activated, down_w, precision=HIGH) + down_b)
        encoded = low(after_attn + mlp_out)
        projected = low(low_back(jnp.dot(encoded, dec_w, precision=HIGH) + dec_b))
        return jnp.where(filled, projected[source], mask_vec) + position_f
    decoded, backward = jax.vjp(forward, patches.astype(jnp.float32), norm1_gain, norm1_bias, qkv_weight.astype(jnp.float32), qv_bias, out_weight.astype(jnp.float32), out_bias, norm2_gain, norm2_bias, up_weight.astype(jnp.float32), up_bias.astype(jnp.float32), down_weight.astype(jnp.float32), down_bias, dec_weight.astype(jnp.float32), dec_bias, mask_token)
    grads = backward(cotangent.astype(jnp.float32))
    return (decoded.astype(jnp.bfloat16), grads[0], grads[1], grads[2], grads[3], grads[4], grads[5], grads[6], grads[7], grads[8], grads[9], grads[10], grads[11], grads[12], grads[13], grads[14], grads[15])
```

```python
import jax
import jax.numpy as jnp
from jax import lax
from jax.sharding import PartitionSpec as P

HEAD_DIM = 64
QBLOCK = 512


NEG_FILL = -1000000000.0


def layer_norm(hidden, gain, bias_vec):
    centered = hidden - jnp.mean(hidden, axis=-1, keepdims=True)
    spread = jnp.mean(centered * centered, axis=-1, keepdims=True)
    return centered * lax.rsqrt(spread + 1e-06) * gain + bias_vec


def gelu_exact(values):
    return jax.nn.gelu(values, approximate=False)


def gather_rows(weight, data_par, model_par):
    rows, width = weight.shape
    part = rows // data_par
    mine = lax.dynamic_slice_in_dim(weight, lax.axis_index("dp") * part, part, 0)
    column = lax.all_gather(mine, "mp", axis=0)
    whole = lax.all_gather(column, "dp", axis=0)
    return whole.transpose(1, 0, 2, 3).reshape(model_par * rows, width)


def low(values):
    return values.astype(jnp.bfloat16)


def per_device(
    patches,
    scene_ids,
    owner_ids,
    fill_slot,
    norm1_gain,
    norm1_bias,
    qkv_weight,
    qv_bias,
    out_weight,
    out_bias,
    norm2_gain,
    norm2_bias,
    up_weight,
    up_bias,
    down_weight,
    down_bias,
    dec_weight,
    dec_bias,
    mask_token,
    positions,
    cotangent,
):
    row_count = patches.shape[0]
    model_par = lax.axis_size("mp")
    data_par = lax.axis_size("dp")
    group_rows = row_count * model_par
    total_rows = float(row_count * model_par * data_par)
    local_width = qkv_weight.shape[2]
    local_heads = local_width // HEAD_DIM
    score_scale = HEAD_DIM ** (-0.5)
    block_rows = min(QBLOCK, group_rows)
    block_starts = jnp.arange(group_rows // block_rows, dtype=jnp.int32) * block_rows
    capacity = 2 * row_count // data_par
    slot_count = capacity * data_par
    dec_width = dec_weight.shape[1]
    out_full = gather_rows(out_weight, data_par, model_par)
    inputs_f = patches.astype(jnp.float32)
    band_sums = lax.psum(
        (jnp.sum(inputs_f, axis=0), jnp.sum(inputs_f * inputs_f, axis=0)), ("dp", "mp")
    )
    band_mean = band_sums[0] / total_rows
    band_var = band_sums[1] / total_rows - band_mean * band_mean
    band_scale = lax.rsqrt(band_var + 1e-05)
    band_hat = (inputs_f - band_mean) * band_scale
    normed1 = layer_norm(band_hat, norm1_gain, norm1_bias).astype(jnp.bfloat16)
    norm1_all, scene_all = (
        lax.all_gather(normed1, "mp", axis=0, tiled=True),
        lax.all_gather(scene_ids, "mp", axis=0, tiled=True),
    )
    bias_three = jnp.stack([qv_bias[0], jnp.zeros_like(qv_bias[0]), qv_bias[1]])
    triples = (
        jnp.einsum("td,dcj->tcj", norm1_all, qkv_weight, preferred_element_type=jnp.float32)
        + bias_three
    ).astype(jnp.bfloat16)
    query_all = triples[:, 0].reshape(group_rows, local_heads, HEAD_DIM)
    key_all = triples[:, 1].reshape(group_rows, local_heads, HEAD_DIM)
    value_all = triples[:, 2].reshape(group_rows, local_heads, HEAD_DIM)

    def block_scores(first_row):
        query_blk = lax.dynamic_slice_in_dim(query_all, first_row, block_rows, 0)
        scene_blk = lax.dynamic_slice_in_dim(scene_all, first_row, block_rows, 0)
        scores = (
            jnp.einsum("qhd,khd->hqk", query_blk, key_all, preferred_element_type=jnp.float32)
            * score_scale
        )
        same_scene = (scene_blk[:, None] == scene_all[None, :])[None]
        return (jnp.where(same_scene, scores, NEG_FILL), query_blk)

    def attend_block(first_row):
        scores, query_blk = block_scores(first_row)
        row_max = jnp.max(scores, axis=-1, keepdims=True)
        exp_scores = jnp.exp(scores - row_max)
        row_total = jnp.sum(exp_scores, axis=-1, keepdims=True)
        softmax_w = (exp_scores / row_total).astype(jnp.bfloat16)
        mixed_rows = jnp.einsum(
            "hqk,khd->qhd", softmax_w, value_all, preferred_element_type=jnp.float32
        )
        return (mixed_rows.astype(jnp.bfloat16), (row_max + jnp.log(row_total))[..., 0])

    head_blocks, lse_blocks = lax.map(attend_block, block_starts)
    heads_out = head_blocks.reshape(group_rows, local_width)
    heads_rows = lax.all_to_all(heads_out, "mp", split_axis=0, concat_axis=1, tiled=True)
    attn_local = jnp.dot(heads_rows, out_full, preferred_element_type=jnp.float32)
    after_attn = band_hat + attn_local + out_bias
    normed2 = layer_norm(after_attn, norm2_gain, norm2_bias).astype(jnp.bfloat16)
    norm2_all = lax.all_gather(normed2, "mp", axis=0, tiled=True)
    pre_act = jnp.dot(norm2_all, up_weight, preferred_element_type=jnp.float32) + up_bias.astype(
        jnp.float32
    )
    act_rows = gelu_exact(pre_act).astype(jnp.bfloat16)
    mlp_part = low(jnp.dot(act_rows, down_weight, preferred_element_type=jnp.float32))
    proj_part = jnp.dot(mlp_part, dec_weight, preferred_element_type=jnp.float32)
    proj_sum = lax.psum_scatter(low(proj_part), "mp", scatter_dimension=0, tiled=True)
    direct = after_attn + down_bias
    projected = low(
        jnp.dot(low(direct), dec_weight, preferred_element_type=jnp.float32)
        + proj_sum.astype(jnp.float32)
        + dec_bias
    )
    owner_onehot = (owner_ids[:, None] == jnp.arange(data_par, dtype=jnp.int32)[None, :]).astype(
        jnp.int32
    )
    earlier = jnp.sum((jnp.cumsum(owner_onehot, axis=0) - owner_onehot) * owner_onehot, axis=1)
    send_slot = owner_ids * capacity + earlier
    slot_range = jnp.arange(slot_count, dtype=jnp.int32)
    send_onehot = (send_slot[:, None] == slot_range[None, :]).astype(jnp.bfloat16)
    outgoing = jnp.einsum(
        "rs,rc->sc", send_onehot, projected, preferred_element_type=jnp.float32
    ).astype(jnp.bfloat16)
    fill_onehot = (fill_slot[:, None] == slot_range[None, :]).astype(jnp.bfloat16)
    returning = jnp.einsum(
        "gs,gc->sc", fill_onehot, cotangent, preferred_element_type=jnp.float32
    ).astype(jnp.bfloat16)
    arrived, grad_back = (
        lax.all_to_all(
            outgoing.reshape(data_par, capacity, dec_width),
            "dp",
            split_axis=0,
            concat_axis=0,
            tiled=True,
        ),
        lax.all_to_all(
            returning.reshape(data_par, capacity, dec_width),
            "dp",
            split_axis=0,
            concat_axis=0,
            tiled=True,
        ),
    )
    placed = jnp.dot(
        fill_onehot, arrived.reshape(slot_count, dec_width), preferred_element_type=jnp.float32
    )
    masked = (fill_slot < 0)[:, None]
    decoder_in = (jnp.where(masked, mask_token, placed) + positions.astype(jnp.float32)).astype(
        jnp.bfloat16
    )
    grad_mask_local = jnp.sum(jnp.where(masked, cotangent.astype(jnp.float32), 0.0), axis=0)
    grad_proj = jnp.einsum(
        "rs,sc->rc",
        send_onehot,
        grad_back.reshape(slot_count, dec_width),
        preferred_element_type=jnp.float32,
    )
    grad_proj_low = grad_proj.astype(jnp.bfloat16)
    proj_grad_all = lax.all_gather(grad_proj_low, "mp", axis=0, tiled=True)
    grad_dec_local = jnp.einsum(
        "rd,rc->dc", low(direct), grad_proj_low, preferred_element_type=jnp.float32
    ) + jnp.einsum("rd,rc->dc", mlp_part, proj_grad_all, preferred_element_type=jnp.float32)
    grad_dec_bias_local = jnp.sum(grad_proj, axis=0)
    grad_block = jnp.einsum(
        "rc,dc->rd", grad_proj_low, dec_weight, preferred_element_type=jnp.float32
    )
    grad_down_bias_local = jnp.sum(low(grad_block).astype(jnp.float32), axis=0)
    grad_mlp_all = low(
        jnp.einsum("rc,dc->rd", proj_grad_all, dec_weight, preferred_element_type=jnp.float32)
    )
    grad_act = jnp.einsum(
        "tc,fc->tf", grad_mlp_all, down_weight, preferred_element_type=jnp.float32
    )
    grad_down_local = jnp.einsum(
        "tf,tc->fc", act_rows, grad_mlp_all, preferred_element_type=jnp.float32
    )
    down_sum = lax.psum(low(grad_down_local), "dp").astype(jnp.float32)
    gelu_val, gelu_back = jax.vjp(gelu_exact, pre_act)
    grad_pre = gelu_back(grad_act)[0].astype(jnp.bfloat16)
    grad_up_local = jnp.einsum("td,tf->df", norm2_all, grad_pre, preferred_element_type=jnp.float32)
    grad_up_bias_local = jnp.sum(grad_pre.astype(jnp.float32), axis=0)
    grad_norm2 = lax.psum_scatter(
        low(jnp.einsum("tf,df->td", grad_pre, up_weight, preferred_element_type=jnp.float32)),
        "mp",
        scatter_dimension=0,
        tiled=True,
    ).astype(jnp.float32)
    up_sum = lax.psum(low(grad_up_local), "dp").astype(jnp.float32)
    norm2_val, norm2_back = jax.vjp(layer_norm, after_attn, norm2_gain, norm2_bias)
    from_norm2, grad_gain2_local, grad_bias2_local = norm2_back(grad_norm2)
    grad_after = grad_block + from_norm2
    grad_attn = grad_after.astype(jnp.bfloat16)
    grad_out_bias_local = jnp.sum(grad_attn.astype(jnp.float32), axis=0)
    grad_out_rows = low(
        jnp.einsum("tj,tc->jc", heads_rows, grad_attn, preferred_element_type=jnp.float32)
    ).reshape(model_par, local_width, -1)
    out_part = lax.psum_scatter(grad_out_rows, "dp", scatter_dimension=1, tiled=True)
    out_part = lax.psum_scatter(out_part, "mp", scatter_dimension=0, tiled=True)
    out_sum = lax.all_gather(out_part[0], "dp", axis=0, tiled=True).astype(jnp.float32)
    grad_heads = lax.all_to_all(
        low(jnp.einsum("tc,jc->tj", grad_attn, out_full, preferred_element_type=jnp.float32)),
        "mp",
        split_axis=1,
        concat_axis=0,
        tiled=True,
    )
    grad_heads3 = grad_heads.reshape(group_rows, local_heads, HEAD_DIM)

    def back_block(carried, inputs):
        key_acc, value_acc = carried
        first_row, log_total = inputs
        scores, query_blk = block_scores(first_row)
        softmax_w = jnp.exp(scores - log_total[..., None])
        upstream = lax.dynamic_slice_in_dim(grad_heads3, first_row, block_rows, 0)
        value_acc = value_acc + jnp.einsum(
            "hqk,qhd->khd",
            softmax_w.astype(jnp.bfloat16),
            upstream,
            preferred_element_type=jnp.float32,
        )
        grad_probs = jnp.einsum(
            "qhd,khd->hqk", upstream, value_all, preferred_element_type=jnp.float32
        )
        inner_sum = jnp.sum(softmax_w * grad_probs, axis=-1, keepdims=True)
        grad_scores = (softmax_w * (grad_probs - inner_sum)).astype(jnp.bfloat16)
        grad_query = (
            jnp.einsum("hqk,khd->qhd", grad_scores, key_all, preferred_element_type=jnp.float32)
            * score_scale
        )
        key_acc = (
            key_acc
            + jnp.einsum("hqk,qhd->khd", grad_scores, query_blk, preferred_element_type=jnp.float32)
            * score_scale
        )
        return ((key_acc, value_acc), grad_query.astype(jnp.bfloat16))

    zero_heads = jnp.zeros((group_rows, local_heads, HEAD_DIM), jnp.float32)
    (key_grad, value_grad), query_blocks = lax.scan(
        back_block, (zero_heads, zero_heads), (block_starts, lse_blocks)
    )
    grad_triples = jnp.stack(
        [
            query_blocks.reshape(group_rows, local_width),
            key_grad.reshape(group_rows, local_width).astype(jnp.bfloat16),
            value_grad.reshape(group_rows, local_width).astype(jnp.bfloat16),
        ],
        axis=1,
    )
    grad_qkv_local = jnp.einsum(
        "td,tcj->dcj", norm1_all, grad_triples, preferred_element_type=jnp.float32
    )
    triple_sums = jnp.sum(grad_triples.astype(jnp.float32), axis=0)
    grad_qv_local = jnp.stack([triple_sums[0], triple_sums[2]])
    grad_norm1 = lax.psum_scatter(
        low(jnp.einsum("tcj,dcj->td", grad_triples, qkv_weight, preferred_element_type=jnp.float32)),
        "mp",
        scatter_dimension=0,
        tiled=True,
    ).astype(jnp.float32)
    qkv_sum = lax.psum(low(grad_qkv_local), "dp").astype(jnp.float32)
    norm1_val, norm1_back = jax.vjp(layer_norm, band_hat, norm1_gain, norm1_bias)
    from_norm1, grad_gain1_local, grad_bias1_local = norm1_back(grad_norm1)
    grad_hat = grad_after + from_norm1
    dec_sum = lax.psum(low(grad_dec_local), ("dp", "mp")).astype(jnp.float32)
    summed_small = lax.psum((grad_qv_local, grad_up_bias_local), "dp")
    shared = lax.psum(
        (
            jnp.sum(grad_hat, axis=0),
            jnp.sum(grad_hat * band_hat, axis=0),
            grad_gain1_local,
            grad_bias1_local,
            grad_gain2_local,
            grad_bias2_local,
            grad_out_bias_local,
            grad_down_bias_local,
            grad_dec_bias_local,
            grad_mask_local,
        ),
        ("dp", "mp"),
    )
    grad_patches = band_scale * (
        grad_hat - shared[0] / total_rows - band_hat * (shared[1] / total_rows)
    )
    return (
        decoder_in,
        grad_patches,
        shared[2],
        shared[3],
        qkv_sum,
        summed_small[0],
        out_sum,
        shared[6],
        shared[4],
        shared[5],
        up_sum,
        summed_small[1],
        down_sum,
        shared[7],
        dec_sum,
        shared[8],
        shared[9],
    )


def solution(mesh):
    in_specs = (
        P(("dp", "mp"), None),
        P(("dp", "mp")),
        P(("dp", "mp")),
        P(("dp", "mp")),
        P(),
        P(),
        P(None, None, "mp"),
        P(None, "mp"),
        P("mp", None),
        P(),
        P(),
        P(),
        P(None, "mp"),
        P("mp"),
        P("mp", None),
        P(),
        P(),
        P(),
        P(),
        P(("dp", "mp"), None),
        P(("dp", "mp"), None),
    )
    out_specs = (
        P(("dp", "mp"), None),
        P(("dp", "mp"), None),
        P(),
        P(),
        P(None, None, "mp"),
        P(None, "mp"),
        P("mp", None),
        P(),
        P(),
        P(),
        P(None, "mp"),
        P("mp"),
        P("mp", None),
        P(),
        P(),
        P(),
        P(),
    )
    return jax.shard_map(
        per_device, mesh=mesh, in_specs=in_specs, out_specs=out_specs, check_vma=False
    )
```
